512 devices in a mesh: tm: 32 (over x_lo, z), height: 16 (over x_hi, y, core).
Axes of the slice: x: 4 (x_hi: 2, x_lo: 2; x = x_hi * 2 + x_lo), y: 4, z: 16, core: 2. Of those that a mesh axis runs over, the one named last changes fastest.
Arguments:
- query_vecs: bfloat16 [32, 16, 128, 1536], P('tm', 'height'), may hold values from -8 to 8
- key_vecs: bfloat16 [32, 16, 128, 1536], P('tm', 'height'), may hold values from -8 to 8
- value_vecs: bfloat16 [32, 16, 128, 1536], P('tm', 'height'), may hold values from -6 to 6
- grad_output: bfloat16 [32, 16, 128, 1536], P('tm', 'height'), may hold values from -6 to 6
- tile_window: int32 [12, 3], replicated, may hold values from 0 to 1, as said below
- neighbour_mask: int32 [12, 27], replicated, may hold values from 0 to 1, as said below
Outputs:
- attended: bfloat16 [32, 16, 128, 1536], P('tm', 'height')
- grad_query: bfloat16 [32, 16, 128, 1536], P('tm', 'height')
- grad_key: bfloat16 [32, 16, 128, 1536], P('tm', 'height')
- grad_value: bfloat16 [32, 16, 128, 1536], P('tm', 'height')
The draws below stay inside these ranges and needn't reach their ends.
Inputs may be any that keep to these rules, and one draw needn't show every extreme that they name: `tile_window`: in each of the three columns exactly half of the 12 heads have 1 and the others 0. `neighbour_mask`: entry 13 (no offset) is 1 for every head.
All inputs are finite; a program needn't handle non-finite values.
Results may differ from the reference program's by a relative error of at most 0.025.
Values may be sent and summed in bfloat16 or wider, within the bound.
A program may use at most 64 MiB of HBM per device.

```python
import math
import jax
import jax.numpy as jnp
from jax import lax

HEADS = 12
TILE = 32
SLAB = 128
FEAT = 1536
TM_TILES = 32
HT_TILES = 16


def draw_query_vecs(key, part):
    shape = (TM_TILES, HT_TILES, SLAB, FEAT)
    own_key = jax.random.fold_in(key, 11)
    result = jnp.clip(jax.random.normal(own_key, shape), -6.0, 6.0)
    return result.astype(jnp.bfloat16)


def draw_key_vecs(key, part):
    shape = (TM_TILES, HT_TILES, SLAB, FEAT)
    own_key = jax.random.fold_in(key, 23)
    result = jnp.clip(jax.random.normal(own_key, shape), -6.0, 6.0)
    return result.astype(jnp.bfloat16)


def draw_tile_window(key, part):
    columns = []
    for axis_number in range(3):
        order = jax.random.permutation(jax.random.fold_in(key, 31 + axis_number), HEADS)
        columns.append(jnp.where(order < HEADS // 2, 1, 0).astype(jnp.int32))
    return jnp.stack(columns, axis=1)


def draw_neighbour_mask(key, part):
    levels = jax.random.randint(jax.random.fold_in(key, 53), (HEADS, 27), 0, 4)
    centre = jnp.arange(27, dtype=jnp.int32) == 13
    return jnp.where(centre[None, :] | (levels > 0), 1, 0).astype(jnp.int32)


def block_scale(stream_key, dims, cuts, smallest, top_value):
    factor_of = 1.0
    for position, shards_of in cuts:
        steps = jax.random.uniform(jax.random.fold_in(jax.random.fold_in(stream_key, 6), position), (shards_of,), jnp.float32, smallest / len(cuts), top_value / len(cuts))
        factor_of = factor_of * jnp.repeat(jnp.exp(steps), dims[position] // shards_of).reshape((-1,) + (1,) * (len(dims) - 1 - position))
    return factor_of


def bell_draw(key, dims, deviation, most, cuts=(), kind=jnp.bfloat16):
    values = deviation * jax.random.normal(key, dims, jnp.float32)
    if cuts:
        values = values * block_scale(key, dims, cuts, -0.22, 0.18)
    return jnp.clip(values, -most, most).astype(kind)


def setup_inputs(seed: int = 0) -> dict:
    seeds = jax.random.split(jax.random.key(seed), 7)
    query_vecs = draw_query_vecs(jax.random.fold_in(seeds[6], 71), 0)
    key_vecs = draw_key_vecs(jax.random.fold_in(seeds[6], 71), 0)
    value_vecs = bell_draw(seeds[2], (TM_TILES, HT_TILES, SLAB, FEAT), 1.0, 6.0, ((0, 32), (1, 16)))
    grad_output = bell_draw(seeds[3], (TM_TILES, HT_TILES, SLAB, FEAT), 1.0, 6.0, ((0, 32), (1, 16)))
    tile_window = draw_tile_window(jax.random.fold_in(seeds[6], 71), 0)
    neighbour_mask = draw_neighbour_mask(jax.random.fold_in(seeds[6], 71), 0)
    return {"query_vecs": query_vecs, "key_vecs": key_vecs, "value_vecs": value_vecs, "grad_output": grad_output, "tile_window": tile_window, "neighbour_mask": neighbour_mask}


NEG_LARGE = -1e+30

def contract(left, right, left_dim, right_dim):
    return lax.dot_general(left.astype(jnp.float32), right.astype(jnp.float32), (((left_dim,), (right_dim,)), ((), ())), preferred_element_type=jnp.float32)

def tile_coords(tile_count):
    counter = jnp.arange(9 * tile_count, dtype=jnp.int32)
    outer_t = counter // (3 * tile_count) - 1
    outer_h = counter // tile_count % 3 - 1
    outer_c = counter % tile_count
    inner_c = jnp.arange(tile_count, dtype=jnp.int32)
    return (outer_t, outer_h, outer_c, inner_c)

def pair_table(window_row, mask_row, step_t, step_h, step_w, inside):
    reach = (jnp.abs(step_t) <= window_row[0]) & (jnp.abs(step_h) <= window_row[1]) & (jnp.abs(step_w) <= window_row[2])
    offset = 9 * (step_t + 1) + 3 * (step_h + 1) + jnp.clip(step_w, -1, 1) + 1
    listed = lax.optimization_barrier(jnp.sum(jnp.where(offset[..., None] == jnp.arange(27, dtype=jnp.int32), mask_row, 0), axis=-1))
    return reach & (listed > 0) & inside

def expand_table(tile_table):
    return jnp.repeat(jnp.repeat(tile_table, TILE, axis=0), TILE, axis=1)

def forward_block(query_loc, key_ext, value_ext, grad_loc, time_pos, height_pos, time_count, height_count, tile_window, neighbour_mask):
    slab_len, features = query_loc.shape
    head_count = tile_window.shape[0]
    head_width = features // head_count
    tile_count = slab_len // TILE
    scaling = 1.0 / math.sqrt(head_width)
    outer_t, outer_h, outer_c, inner_c = tile_coords(tile_count)
    inside = (time_pos + outer_t >= 0) & (time_pos + outer_t < time_count) & (height_pos + outer_h >= 0) & (height_pos + outer_h < height_count)
    step_t = jnp.broadcast_to(outer_t[None, :], (tile_count, 9 * tile_count))
    step_h = jnp.broadcast_to(outer_h[None, :], (tile_count, 9 * tile_count))
    step_w = outer_c[None, :] - inner_c[:, None]

    def one_head(number, carried):
        attended, grad_query, log_sums, deltas = carried
        number = number.astype(jnp.int32)
        allowed = expand_table(pair_table(tile_window[number], neighbour_mask[number], step_t, step_h, step_w, inside[None, :]))
        start = number * head_width
        query_head = lax.dynamic_slice_in_dim(query_loc, start, head_width, 1)
        key_head = lax.dynamic_slice_in_dim(key_ext, start, head_width, 1)
        value_head = lax.dynamic_slice_in_dim(value_ext, start, head_width, 1)
        grad_head = lax.dynamic_slice_in_dim(grad_loc, start, head_width, 1)
        scores = jnp.where(allowed, contract(query_head, key_head, 1, 1) * scaling, NEG_LARGE)
        highest = lax.optimization_barrier(jnp.max(scores, axis=1, keepdims=True))
        log_sum = highest[:, 0] + jnp.log(lax.optimization_barrier(jnp.sum(jnp.exp(scores - highest), axis=1)))
        probs_high = jnp.exp(scores - log_sum[:, None])
        probs_low = probs_high.astype(jnp.bfloat16)
        out_head = contract(probs_low, value_head, 1, 0).astype(jnp.bfloat16)
        delta_row = lax.optimization_barrier(jnp.sum(grad_head.astype(jnp.float32) * out_head.astype(jnp.float32), axis=1))
        grad_probs = contract(grad_head, value_head, 1, 1)
        grad_scores = (probs_high * (grad_probs - delta_row[:, None])).astype(jnp.bfloat16)
        grad_piece = (contract(grad_scores, key_head, 1, 0) * scaling).astype(jnp.bfloat16)
        attended = lax.dynamic_update_slice_in_dim(attended, out_head, start, 1)
        grad_query = lax.dynamic_update_slice_in_dim(grad_query, grad_piece, start, 1)
        log_sums = lax.dynamic_update_slice_in_dim(log_sums, log_sum[None, :], number, 0)
        deltas = lax.dynamic_update_slice_in_dim(deltas, delta_row[None, :], number, 0)
        return (attended, grad_query, log_sums, deltas)
    initial = (jnp.zeros((slab_len, features), jnp.bfloat16), jnp.zeros((slab_len, features), jnp.bfloat16), jnp.zeros((head_count, slab_len), jnp.float32), jnp.zeros((head_count, slab_len), jnp.float32))
    return lax.fori_loop(0, head_count, one_head, initial)

def backward_block(query_ext, grad_ext, sums_ext, deltas_ext, key_loc, value_loc, time_pos, height_pos, time_count, height_count, tile_window, neighbour_mask):
    slab_len, features = key_loc.shape
    head_count = tile_window.shape[0]
    head_width = features // head_count
    tile_count = slab_len // TILE
    scaling = 1.0 / math.sqrt(head_width)
    outer_t, outer_h, outer_c, inner_c = tile_coords(tile_count)
    inside = (time_pos + outer_t >= 0) & (time_pos + outer_t < time_count) & (height_pos + outer_h >= 0) & (height_pos + outer_h < height_count)
    step_t = jnp.broadcast_to(-outer_t[:, None], (9 * tile_count, tile_count))
    step_h = jnp.broadcast_to(-outer_h[:, None], (9 * tile_count, tile_count))
    step_w = inner_c[None, :] - outer_c[:, None]

    def one_head(number, carried):
        grad_key, grad_value = carried
        number = number.astype(jnp.int32)
        allowed = expand_table(pair_table(tile_window[number], neighbour_mask[number], step_t, step_h, step_w, inside[:, None]))
        start = number * head_width
        query_head = lax.dynamic_slice_in_dim(query_ext, start, head_width, 1)
        grad_head = lax.dynamic_slice_in_dim(grad_ext, start, head_width, 1)
        key_head = lax.dynamic_slice_in_dim(key_loc, start, head_width, 1)
        value_head = lax.dynamic_slice_in_dim(value_loc, start, head_width, 1)
        sum_row = lax.dynamic_index_in_dim(sums_ext, number, 0, keepdims=False)
        delta_row = lax.dynamic_index_in_dim(deltas_ext, number, 0, keepdims=False)
        scores = jnp.where(allowed, contract(query_head, key_head, 1, 1) * scaling, NEG_LARGE)
        probs_high = jnp.exp(scores - sum_row[:, None])
        probs_low = probs_high.astype(jnp.bfloat16)
        value_piece = contract(probs_low, grad_head, 0, 0).astype(jnp.bfloat16)
        grad_probs = contract(grad_head, value_head, 1, 1)
        grad_scores = (probs_high * (grad_probs - delta_row[:, None])).astype(jnp.bfloat16)
        key_piece = (contract(grad_scores, query_head, 0, 0) * scaling).astype(jnp.bfloat16)
        grad_key = lax.dynamic_update_slice_in_dim(grad_key, key_piece, start, 1)
        grad_value = lax.dynamic_update_slice_in_dim(grad_value, value_piece, start, 1)
        return (grad_key, grad_value)
    initial = (jnp.zeros((slab_len, features), jnp.bfloat16), jnp.zeros((slab_len, features), jnp.bfloat16))
    return lax.fori_loop(0, head_count, one_head, initial)

def padded(array):
    return jnp.pad(array, ((1, 1), (1, 1), (0, 0), (0, 0)))

def arrange(result):
    return result.reshape((TM_TILES, HT_TILES) + result.shape[2:])

def reference(query_vecs, key_vecs, value_vecs, grad_output, tile_window, neighbour_mask):
    block_count = TM_TILES * HT_TILES
    group_size = math.gcd(block_count, 16)
    numbers = jnp.arange(block_count, dtype=jnp.int32).reshape(block_count // group_size, group_size)
    key_pad = padded(key_vecs)
    value_pad = padded(value_vecs)

    def first_pass(number):
        time_pos = (number // HT_TILES).astype(jnp.int32)
        height_pos = (number % HT_TILES).astype(jnp.int32)
        zero_idx = time_pos * 0
        corner = (time_pos, height_pos, zero_idx, zero_idx)
        key_ext = lax.dynamic_slice(key_pad, corner, (3, 3, SLAB, FEAT)).reshape(9 * SLAB, FEAT)
        value_ext = lax.dynamic_slice(value_pad, corner, (3, 3, SLAB, FEAT)).reshape(9 * SLAB, FEAT)
        query_loc = lax.dynamic_slice(query_vecs, corner, (1, 1, SLAB, FEAT)).reshape(SLAB, FEAT)
        grad_loc = lax.dynamic_slice(grad_output, corner, (1, 1, SLAB, FEAT)).reshape(SLAB, FEAT)
        return forward_block(query_loc, key_ext, value_ext, grad_loc, time_pos, height_pos, TM_TILES, HT_TILES, tile_window, neighbour_mask)
    attended, grad_query, log_sums, deltas = lax.map(jax.vmap(first_pass), numbers)
    attended = arrange(attended)
    grad_query = arrange(grad_query)
    sums_pad = padded(arrange(log_sums))
    deltas_pad = padded(arrange(deltas))
    query_pad = padded(query_vecs)
    grad_pad = padded(grad_output)
    head_count = tile_window.shape[0]

    def second_pass(number):
        time_pos = (number // HT_TILES).astype(jnp.int32)
        height_pos = (number % HT_TILES).astype(jnp.int32)
        zero_idx = time_pos * 0
        corner = (time_pos, height_pos, zero_idx, zero_idx)
        query_ext = lax.dynamic_slice(query_pad, corner, (3, 3, SLAB, FEAT)).reshape(9 * SLAB, FEAT)
        grad_ext = lax.dynamic_slice(grad_pad, corner, (3, 3, SLAB, FEAT)).reshape(9 * SLAB, FEAT)
        sums_ext = lax.dynamic_slice(sums_pad, corner, (3, 3, head_count, SLAB)).transpose(2, 0, 1, 3).reshape(head_count, 9 * SLAB)
        deltas_ext = lax.dynamic_slice(deltas_pad, corner, (3, 3, head_count, SLAB)).transpose(2, 0, 1, 3).reshape(head_count, 9 * SLAB)
        key_loc = lax.dynamic_slice(key_vecs, corner, (1, 1, SLAB, FEAT)).reshape(SLAB, FEAT)
        value_loc = lax.dynamic_slice(value_vecs, corner, (1, 1, SLAB, FEAT)).reshape(SLAB, FEAT)
        return backward_block(query_ext, grad_ext, sums_ext, deltas_ext, key_loc, value_loc, time_pos, height_pos, TM_TILES, HT_TILES, tile_window, neighbour_mask)
    grad_key, grad_value = lax.map(jax.vmap(second_pass), numbers)
    return (attended, grad_query, arrange(grad_key), arrange(grad_value))
```

```python
import functools
import math

import jax
import jax.numpy as jnp
from jax import lax
from jax.experimental import pallas as pl
from jax.experimental.pallas import tpu as pltpu
from jax.sharding import PartitionSpec as P

TILE = 32
NEG = -1e30
K, V, Q, G = 0, 1, 2, 3
MESH = pl.DeviceIdType.MESH


def dot_nt(a, b):
    return lax.dot_general(a, b, (((1,), (1,)), ((), ())), preferred_element_type=jnp.float32)


def dot_nn(a, b):
    return lax.dot_general(a, b, (((1,), (0,)), ((), ())), preferred_element_type=jnp.float32)


def dot_tn(a, b):
    return lax.dot_general(a, b, (((0,), (0,)), ((), ())), preferred_element_type=jnp.float32)


def fused_kernel(
    n, half, heads, tc, hc, slab, width,
    penalty, own,
    o_out, dq_out, dk_out, dv_out,
    rt, rh, rd, dk_acc, dv_acc, stats_col, stats, stats_in,
    tsend, trecv, hsend, hrecv, dsend, drecv, ssend, srecv,
):
    scale = 1.0 / math.sqrt(width)
    t = lax.axis_index("tm")
    h = lax.axis_index("height")
    rest = half - n
    t_near = (jnp.maximum(t - 1, 0), jnp.minimum(t + 1, tc - 1))
    h_near = (jnp.maximum(h - 1, 0), jnp.minimum(h + 1, hc - 1))
    has_t = (t > 0, t < tc - 1)
    has_h = (h > 0, h < hc - 1)

    barrier = pltpu.get_barrier_semaphore()
    for a in (-1, 0, 1):
        for b in (-1, 0, 1):
            if a == 0 and b == 0:
                continue
            ok = True
            if a != 0:
                ok = has_t[(a + 1) // 2]
            if b != 0:
                ok = jnp.logical_and(ok, has_h[(b + 1) // 2])

            @pl.when(ok)
            def _(a=a, b=b):
                pl.semaphore_signal(barrier, inc=1, device_id=(t + a, h + b), device_id_type=MESH)

    for d in (0, 1):
        @pl.when(jnp.logical_not(has_t[d]))
        def _(d=d):
            rt[d] = jnp.zeros(rt.shape[1:], rt.dtype)

        @pl.when(jnp.logical_not(has_h[d]))
        def _(d=d):
            rh[d] = jnp.zeros(rh.shape[1:], rh.dtype)

        if n:
            for e in (0, 1):
                @pl.when(jnp.logical_not(jnp.logical_and(has_h[d], has_t[e])))
                def _(d=d, e=e):
                    rd[d, e] = jnp.zeros(rd.shape[2:], rd.dtype)

    for a in range(3):
        for b in range(3):
            if a == 1 and b == 1:
                continue
            ok = True
            if a != 1:
                ok = has_t[a // 2]
            if b != 1:
                ok = jnp.logical_and(ok, has_h[b // 2])

            @pl.when(jnp.logical_not(ok))
            def _(a=a, b=b):
                stats_in[a, b] = jnp.zeros(stats_in.shape[2:], jnp.float32)

    count_t = has_t[0].astype(jnp.int32) + has_t[1].astype(jnp.int32)
    count_h = has_h[0].astype(jnp.int32) + has_h[1].astype(jnp.int32)
    pl.semaphore_wait(barrier, count_t + count_h + count_t * count_h)

    parts = []
    if n:
        parts.append((0, 0, n))
    if rest:
        parts.append((1, n, rest))

    def t_copy(array, part, d):
        index, first, size = part
        return pltpu.make_async_remote_copy(
            src_ref=own.at[array, pl.ds(first, size)],
            dst_ref=rt.at[1 - d, array, pl.ds(first, size)],
            send_sem=tsend.at[array, index, d],
            recv_sem=trecv.at[array, index, 1 - d],
            device_id=(t_near[d], h), device_id_type=MESH,
        )

    def h_copy(array, part, d):
        index, first, size = part
        source = 0 if index == 0 else half
        return pltpu.make_async_remote_copy(
            src_ref=own.at[array, pl.ds(source, size)],
            dst_ref=rh.at[1 - d, array, pl.ds(first, size)],
            send_sem=hsend.at[array, index, d],
            recv_sem=hrecv.at[array, index, 1 - d],
            device_id=(t, h_near[d]), device_id_type=MESH,
        )

    def d_copy(array, e, d):
        return pltpu.make_async_remote_copy(
            src_ref=rt.at[e, array, pl.ds(0, n)],
            dst_ref=rd.at[1 - d, e, array],
            send_sem=dsend.at[array, e, d],
            recv_sem=drecv.at[array, e, 1 - d],
            device_id=(t, h_near[d]), device_id_type=MESH,
        )

    for part in parts:
        for array in range(4):
            for d in (0, 1):
                @pl.when(has_t[d])
                def _(part=part, array=array, d=d):
                    t_copy(array, part, d).start()

                @pl.when(has_h[d])
                def _(part=part, array=array, d=d):
                    h_copy(array, part, d).start()

    if n:
        for array in range(4):
            for e in (0, 1):
                @pl.when(has_t[e])
                def _(array=array, e=e):
                    t_copy(array, parts[0], 1 - e).wait_recv()
                    for d in (0, 1):
                        @pl.when(has_h[d])
                        def _(d=d):
                            d_copy(array, e, d).start()

    for part in parts:
        for array in range(4):
            for e in (0, 1):
                if part[0] == 1:
                    @pl.when(has_t[e])
                    def _(part=part, array=array, e=e):
                        t_copy(array, part, 1 - e).wait_recv()

                @pl.when(has_h[e])
                def _(part=part, array=array, e=e):
                    h_copy(array, part, 1 - e).wait_recv()

    if n:
        for array in range(4):
            for d in (0, 1):
                for e in (0, 1):
                    @pl.when(jnp.logical_and(has_h[d], has_t[e]))
                    def _(array=array, d=d, e=e):
                        d_copy(array, e, 1 - d).wait_recv()

    def inside(dt, dr):
        ok = True
        if dt:
            ok = has_t[(dt + 1) // 2]
        if dr:
            ok = jnp.logical_and(ok, has_h[(dr + 1) // 2])
        return ok

    row_tile = lax.broadcasted_iota(jnp.int32, (slab, slab), 0) // TILE
    col_tile = lax.broadcasted_iota(jnp.int32, (slab, slab), 1) // TILE
    step = col_tile - row_tile

    def masked(scores, slot, dt, dr, sign):
        first = 9 * (sign * dt + 1) + 3 * (sign * dr + 1) + 1
        added = jnp.full((slab, slab), NEG, jnp.float32)
        for dw in (-1, 0, 1):
            value = penalty[slot, first + dw]
            if dt or dr:
                value = jnp.where(inside(dt, dr), value, NEG)
            added = jnp.where(step == sign * dw, value, added)
        return scores * scale + added

    def block(dt, dr, array, slot):
        if dr == 0:
            return rt[(dt + 1) // 2, array, slot]
        if dt == 0:
            return rh[(dr + 1) // 2, array, slot]
        return rd[(dr + 1) // 2, (dt + 1) // 2, array, slot]

    lane = lax.broadcasted_iota(jnp.int32, (slab, slab), 1)
    stats_col[...] = jnp.zeros((slab, slab), jnp.float32)

    def first_pass(slot, at, offsets):
        query = own[Q, slot]
        cot = own[G, slot]

        def get(array, dt, dr):
            if dt == 0 and dr == 0:
                return own[array, slot]
            return block(dt, dr, array, at)

        scores = []
        for dt, dr in offsets:
            scores.append(masked(dot_nt(query, get(K, dt, dr)), slot, dt, dr, 1))
        highest = scores[0]
        for part in scores[1:]:
            highest = jnp.maximum(highest, part)
        highest = jnp.max(highest, axis=1, keepdims=True)
        weights = [jnp.exp(part - highest) for part in scores]
        total = weights[0]
        for part in weights[1:]:
            total = total + part
        total = jnp.sum(total, axis=1, keepdims=True)
        inverse = 1.0 / total
        out = jnp.zeros((slab, width), jnp.float32)
        probs = []
        for (dt, dr), part in zip(offsets, weights):
            prob = part * inverse
            probs.append(prob)
            out = out + dot_nn(prob.astype(jnp.bfloat16), get(V, dt, dr))
        out = out.astype(jnp.bfloat16)
        o_out[slot] = out
        delta = jnp.sum(cot.astype(jnp.float32) * out.astype(jnp.float32), axis=1, keepdims=True)
        grad = jnp.zeros((slab, width), jnp.float32)
        for (dt, dr), prob in zip(offsets, probs):
            slope = dot_nt(cot, get(V, dt, dr))
            slope = (prob * (slope - delta)).astype(jnp.bfloat16)
            grad = grad + dot_nn(slope, get(K, dt, dr))
            if dt == 0 and dr == 0:
                dk_acc[slot] = dot_tn(slope, query)
                dv_acc[slot] = dot_tn(prob.astype(jnp.bfloat16), cot)
        dq_out[slot] = (grad * scale).astype(jnp.bfloat16)
        log_sum = highest + jnp.log(total)
        held = jnp.where(lane == slot, log_sum, stats_col[...])
        stats_col[...] = jnp.where(lane == slot + 16, delta, held)

    centre = [(0, 0)]
    t_only = [(-1, 0), (1, 0)]
    h_only = [(0, -1), (0, 1)]
    corners = [(-1, -1), (-1, 1), (1, -1), (1, 1)]

    def loop(count, body):
        if count:
            lax.fori_loop(0, count, lambda i, c: (body(i), c)[1], 0)

    loop(n, lambda i: first_pass(i, i, centre + t_only + h_only + corners))
    loop(rest, lambda i: first_pass(n + i, n + i, centre + t_only))
    loop(rest, lambda i: first_pass(half + i, n + i, centre + h_only))
    loop(n, lambda i: first_pass(half + rest + i, 0, centre))

    stats[...] = jnp.transpose(stats_col[...])[: stats.shape[0]]

    def s_copy(a, b):
        return pltpu.make_async_remote_copy(
            src_ref=stats,
            dst_ref=stats_in.at[1 - a, 1 - b],
            send_sem=ssend.at[a + 1, b + 1],
            recv_sem=srecv.at[1 - a, 1 - b],
            device_id=(t_near[(a + 1) // 2] if a else t, h_near[(b + 1) // 2] if b else h),
            device_id_type=MESH,
        )

    near = t_only + h_only + corners
    for a, b in near:
        @pl.when(inside(a, b))
        def _(a=a, b=b):
            s_copy(a, b).start()
    for a, b in near:
        @pl.when(inside(a, b))
        def _(a=a, b=b):
            s_copy(-a, -b).wait_recv()

    def second_pass(slot, at, offsets):
        key = own[K, slot]
        val = own[V, slot]
        dk = dk_acc[slot]
        dv = dv_acc[slot]
        for dt, dr in offsets:
            query = block(dt, dr, Q, at)
            cot = block(dt, dr, G, at)
            log_sum = stats_in[dt + 1, dr + 1, pl.ds(slot, 1), :]
            delta = stats_in[dt + 1, dr + 1, pl.ds(slot + 16, 1), :]
            part = masked(dot_nt(key, query), slot, dt, dr, -1)
            prob = jnp.exp(part - log_sum)
            dv = dv + dot_nn(prob.astype(jnp.bfloat16), cot)
            slope = dot_nt(val, cot)
            slope = (prob * (slope - delta)).astype(jnp.bfloat16)
            dk = dk + dot_nn(slope, query)
        dk_out[slot] = (dk * scale).astype(jnp.bfloat16)
        dv_out[slot] = dv.astype(jnp.bfloat16)

    loop(n, lambda i: second_pass(i, i, near))
    loop(rest, lambda i: second_pass(n + i, n + i, t_only))
    loop(rest, lambda i: second_pass(half + i, n + i, h_only))
    loop(n, lambda i: second_pass(half + rest + i, 0, []))

    for part in parts:
        for array in range(4):
            for d in (0, 1):
                @pl.when(has_t[d])
                def _(part=part, array=array, d=d):
                    t_copy(array, part, d).wait_send()

                @pl.when(has_h[d])
                def _(part=part, array=array, d=d):
                    h_copy(array, part, d).wait_send()
    if n:
        for array in range(4):
            for e in (0, 1):
                for d in (0, 1):
                    @pl.when(jnp.logical_and(has_h[d], has_t[e]))
                    def _(array=array, d=d, e=e):
                        d_copy(array, e, d).wait_send()
    for a, b in near:
        @pl.when(inside(a, b))
        def _(a=a, b=b):
            s_copy(a, b).wait_send()


def pack_kernel(
    heads, width, window, mask, k_in, v_in, q_in, g_in, packed, penalty, slots
):
    half = heads // 2
    time = [window[i, 0] for i in range(heads)]
    height = [window[i, 1] for i in range(heads)]
    both = [x * y for x, y in zip(time, height)]
    total = functools.reduce(lambda x, y: x + y, both)
    seen = [0, total, half, 2 * half - total]
    for i in range(heads):
        kind = [both[i], time[i] - both[i], height[i] - both[i], 1 - time[i] - height[i] + both[i]]
        slot = sum(k * c for k, c in zip(kind, seen))
        seen = [c + k for k, c in zip(kind, seen)]
        slots[i] = slot
        for number, ref in ((K, k_in), (V, v_in), (Q, q_in), (G, g_in)):
            packed[number, slot] = ref[:, i * width : (i + 1) * width]
        for offset in range(27):
            allowed = mask[i, offset] == 1
            for axis, moved in enumerate((offset // 9 != 1, offset // 3 % 3 != 1, offset % 3 != 1)):
                if moved:
                    allowed = jnp.logical_and(allowed, window[i, axis] == 1)
            penalty[slot, offset] = jnp.where(allowed, 0.0, NEG).astype(jnp.float32)


def spread_kernel(heads, width, slots, o_in, dq_in, dk_in, dv_in, o_out, dq_out, dk_out, dv_out):
    for source, target in ((o_in, o_out), (dq_in, dq_out), (dk_in, dk_out), (dv_in, dv_out)):
        for i in range(heads):
            target[:, i * width : (i + 1) * width] = source[slots[i]]


def on_device(tc, hc, query_vecs, key_vecs, value_vecs, grad_output, tile_window, neighbour_mask):
    slab, features = query_vecs.shape[2:]
    heads = tile_window.shape[0]
    half = heads // 2
    width = features // heads
    both = jnp.sum(tile_window[:, 0] * tile_window[:, 1])
    vmem = pl.BlockSpec(memory_space=pltpu.VMEM)
    smem = pl.BlockSpec(memory_space=pltpu.SMEM)
    packed = jax.ShapeDtypeStruct((heads, slab, width), jnp.bfloat16)
    dma = pltpu.SemaphoreType.DMA

    def branch(n):
        def run(penalty, own):
            return pl.pallas_call(
                functools.partial(fused_kernel, n, half, heads, tc, hc, slab, width),
                out_shape=(packed,) * 4,
                in_specs=[smem, vmem],
                out_specs=(vmem,) * 4,
                scratch_shapes=[
                    pltpu.VMEM((2, 4, half, slab, width), jnp.bfloat16),
                    pltpu.VMEM((2, 4, half, slab, width), jnp.bfloat16),
                    pltpu.VMEM((2, 2, 4, max(n, 1), slab, width), jnp.bfloat16),
                    pltpu.VMEM((heads, slab, width), jnp.float32),
                    pltpu.VMEM((heads, slab, width), jnp.float32),
                    pltpu.VMEM((slab, slab), jnp.float32),
                    pltpu.VMEM((32, slab), jnp.float32),
                    pltpu.VMEM((3, 3, 32, slab), jnp.float32),
                    dma((4, 2, 2)), dma((4, 2, 2)),
                    dma((4, 2, 2)), dma((4, 2, 2)),
                    dma((4, 2, 2)), dma((4, 2, 2)),
                    dma((3, 3)), dma((3, 3)),
                ],
                compiler_params=pltpu.CompilerParams(
                    collective_id=n, has_side_effects=True, vmem_limit_bytes=60 * 1024 * 1024
                ),
                name=f"tiles_{n}",
            )(penalty, own)
        return run

    arrays = [x.reshape(slab, features) for x in (key_vecs, value_vecs, query_vecs, grad_output)]
    own, penalty, slots = pl.pallas_call(
        functools.partial(pack_kernel, heads, width),
        out_shape=(
            jax.ShapeDtypeStruct((4, heads, slab, width), jnp.bfloat16),
            jax.ShapeDtypeStruct((heads, 27), jnp.float32),
            jax.ShapeDtypeStruct((heads,), jnp.int32),
        ),
        in_specs=[smem, smem] + [vmem] * 4,
        out_specs=(vmem, smem, smem),
        name="pack",
    )(tile_window, neighbour_mask, *arrays)
    results = lax.switch(both, [branch(n) for n in range(half + 1)], penalty, own)
    flat = jax.ShapeDtypeStruct((slab, features), jnp.bfloat16)
    outs = pl.pallas_call(
        functools.partial(spread_kernel, heads, width),
        out_shape=(flat,) * 4,
        in_specs=[smem] + [vmem] * 4,
        out_specs=(vmem,) * 4,
        name="spread",
    )(slots, *results)
    return tuple(x.reshape(1, 1, slab, features) for x in outs)


def solution(mesh):
    split = P("tm", "height", None, None)
    return jax.shard_map(
        functools.partial(on_device, mesh.shape["tm"], mesh.shape["height"]),
        mesh=mesh,
        in_specs=(split,) * 4 + (P(), P()),
        out_specs=(split,) * 4,
        check_vma=False,
    )
```

```python
import functools
import math

import jax
import jax.numpy as jnp
from jax import lax
from jax.experimental import pallas as pl
from jax.experimental.pallas import tpu as pltpu
from jax.sharding import PartitionSpec as P

TILE = 32
NEG = -1e30
K, V, Q, G = 0, 1, 2, 3
MESH = pl.DeviceIdType.MESH
LOG2E = 1.0 / math.log(2.0)


def dot_nt(a, b):
    return lax.dot_general(a, b, (((1,), (1,)), ((), ())), preferred_element_type=jnp.float32)


def dot_nn(a, b):
    return lax.dot_general(a, b, (((1,), (0,)), ((), ())), preferred_element_type=jnp.float32)


def fused_kernel(
    n, rest, alone, tc, hc, slab, width,
    penalty, own,
    o_out, dq_out, dk_out, dv_out,
    xb, xt, xh, stats_col, stats, stats_in,
    lsend, esend, zsend, tsend, trecv, hsend, hrecv, dsend, drecv, ssend, srecv,
):
    scale = 1.0 / math.sqrt(width)
    half = n + rest
    t = lax.axis_index("tm")
    h = lax.axis_index("height")
    t_near = (jnp.maximum(t - 1, 0), jnp.minimum(t + 1, tc - 1))
    h_near = (jnp.maximum(h - 1, 0), jnp.minimum(h + 1, hc - 1))
    has_t = (t > 0, t < tc - 1)
    has_h = (h > 0, h < hc - 1)
    centre = [(0, 0)]
    t_line = [(-1, 0), (0, 0), (1, 0)]
    h_line = [(0, -1), (0, 0), (0, 1)]
    square = [(dt, dr) for dt in (-1, 0, 1) for dr in (-1, 0, 1)]
    around = [x for x in square if x != (0, 0)]

    def inside(dt, dr):
        ok = True
        if dt:
            ok = has_t[(dt + 1) // 2]
        if dr:
            ok = jnp.logical_and(ok, has_h[(dr + 1) // 2])
        return ok

    def when(ok, body):
        if ok is True:
            body()
        else:
            pl.when(ok)(body)

    cross = {-1: h == hc // 2, 1: h == hc // 2 - 1}
    outer = jnp.logical_or(t == 0, t == tc - 1)
    inner = {-1: t == 1, 1: t == tc - 2}
    near_end = jnp.logical_or(inner[-1], inner[1])

    def both_of(a, b):
        return b if a is True else jnp.logical_and(a, b)

    barrier = pltpu.get_barrier_semaphore()
    for dt, dr in around:
        def greet(dt=dt, dr=dr):
            pl.semaphore_signal(barrier, inc=1, device_id=(t + dt, h + dr), device_id_type=MESH)
        when(inside(dt, dr), greet)

    local = []
    if n:
        local.append(pltpu.make_async_copy(own.at[:, pl.ds(0, n)], xb.at[:, :, 4], lsend.at[0]))
    if rest:
        local.append(pltpu.make_async_copy(own.at[:, pl.ds(n, rest)], xt.at[:, :, 1], lsend.at[1]))
        local.append(pltpu.make_async_copy(own.at[:, pl.ds(half, rest)], xh.at[:, :, 1], lsend.at[2]))
    for copy in local:
        copy.start()

    fill = []
    for dt, dr in around:
        def add(source, target, number, dt=dt, dr=dr):
            copy = pltpu.make_async_copy(source, target, esend.at[number])
            fill.append((jnp.logical_not(inside(dt, dr)), copy))
        if n:
            add(own.at[:, pl.ds(0, n)], xb.at[:, :, 3 * (dt + 1) + dr + 1], 3 * (dt + 1) + dr + 1)
        if rest and dr == 0:
            add(own.at[:, pl.ds(n, rest)], xt.at[:, :, dt + 1], 10 + dt)
        if rest and dt == 0:
            add(own.at[:, pl.ds(half, rest)], xh.at[:, :, dr + 1], 13 + dr)

        def clear(dt=dt, dr=dr):
            stats_in[dt + 1, dr + 1] = jnp.zeros(stats_in.shape[2:], jnp.float32)
        when(jnp.logical_not(inside(dt, dr)), clear)
    for ok, copy in fill:
        when(ok, copy.start)
    stats_col[...] = jnp.zeros((slab, slab), jnp.float32)

    count_t = has_t[0].astype(jnp.int32) + has_t[1].astype(jnp.int32)
    count_h = has_h[0].astype(jnp.int32) + has_h[1].astype(jnp.int32)
    pl.semaphore_wait(barrier, count_t + count_h + count_t * count_h)

    def t_copy(array, part, d):
        if part == 0:
            source, target = own.at[array, pl.ds(0, n)], xb.at[array, :, 3 * (1 - d) + 1]
        else:
            source, target = own.at[array, pl.ds(n, rest)], xt.at[array, :, 1 - d]
        return pltpu.make_async_remote_copy(
            src_ref=source, dst_ref=target,
            send_sem=tsend.at[array, part, d + 1], recv_sem=trecv.at[array, part, 1 - d],
            device_id=(t_near[(d + 1) // 2], h), device_id_type=MESH,
        )

    def h_copy(array, part, d):
        if part == 0:
            source, target = own.at[array, pl.ds(0, n)], xb.at[array, :, 3 + 1 - d]
        else:
            source, target = own.at[array, pl.ds(half, rest)], xh.at[array, :, 1 - d]
        return pltpu.make_async_remote_copy(
            src_ref=source, dst_ref=target,
            send_sem=hsend.at[array, part, d + 1], recv_sem=hrecv.at[array, part, 1 - d],
            device_id=(t, h_near[(d + 1) // 2]), device_id_type=MESH,
        )

    def d_copy(array, e, d):
        return pltpu.make_async_remote_copy(
            src_ref=xb.at[array, :, 3 * (e + 1) + 1], dst_ref=xb.at[array, :, 3 * (e + 1) + 1 - d],
            send_sem=dsend.at[array, e + 1, d + 1], recv_sem=drecv.at[array, e + 1, 1 - d],
            device_id=(t, h_near[(d + 1) // 2]), device_id_type=MESH,
        )

    def z_copy(array, f, d):
        return pltpu.make_async_remote_copy(
            src_ref=xb.at[array, :, 4 + d], dst_ref=xb.at[array, :, 3 * (1 - f) + 1 + d],
            send_sem=zsend.at[array], recv_sem=drecv.at[array, 1 - f, d + 1],
            device_id=(t_near[(f + 1) // 2], h), device_id_type=MESH,
        )

    def s_copy(group, dt, dr):
        return pltpu.make_async_remote_copy(
            src_ref=stats.at[group], dst_ref=stats_in.at[1 - dt, 1 - dr, group],
            send_sem=ssend.at[group, dt + 1, dr + 1], recv_sem=srecv.at[group, 1 - dt, 1 - dr],
            device_id=(t_near[(dt + 1) // 2] if dt else t, h_near[(dr + 1) // 2] if dr else h),
            device_id_type=MESH,
        )

    both, lone = n > 0, rest > 0

    def t_start(array, part):
        for d in (-1, 1):
            when(inside(d, 0), lambda d=d: t_copy(array, part, d).start())

    def h_start(array, part, ok=True):
        for d in (-1, 1):
            when(both_of(ok, inside(0, d)), lambda d=d: h_copy(array, part, d).start())

    def t_wait(array, part):
        for e in (-1, 1):
            when(inside(e, 0), lambda e=e: t_copy(array, part, -e).wait_recv())

    def h_wait(array, part):
        for e in (-1, 1):
            ok = inside(0, e)
            if part == 0:
                ok = both_of(ok, jnp.logical_not(jnp.logical_and(near_end, cross[e])))
            when(ok, lambda e=e: h_copy(array, part, -e).wait_recv())

    def z_relay(array):
        for d in (-1, 1):
            for f in (-1, 1):
                def forward(d=d, f=f):
                    h_copy(array, 0, -d).wait_recv()
                    z_copy(array, f, d).start()
                when(jnp.logical_and(inner[f], cross[d]), forward)

    def relay(array):
        for e in (-1, 1):
            def forward(e=e):
                t_copy(array, 0, -e).wait_recv()
                for d in (-1, 1):
                    ok = jnp.logical_and(inside(0, d), jnp.logical_not(jnp.logical_and(outer, cross[d])))
                    when(ok, lambda d=d: d_copy(array, e, d).start())
            when(inside(e, 0), forward)

    def d_wait(array):
        for e in (-1, 1):
            for d in (-1, 1):
                when(inside(e, d), lambda e=e, d=d: d_copy(array, e, -d).wait_recv())

    def s_start(group, steps):
        for dt, dr in steps:
            when(inside(dt, dr), lambda dt=dt, dr=dr: s_copy(group, dt, dr).start())

    def s_wait(group, steps):
        for dt, dr in steps:
            when(inside(dt, dr), lambda dt=dt, dr=dr: s_copy(group, -dt, -dr).wait_recv())

    row_tile = lax.broadcasted_iota(jnp.int32, (slab, slab), 0) // TILE
    col_tile = lax.broadcasted_iota(jnp.int32, (slab, slab), 1) // TILE
    step = col_tile - row_tile
    lane = lax.broadcasted_iota(jnp.int32, (slab, slab), 1)

    def added(slot, dt, dr, sign, minus=None):
        first = 9 * (sign * dt + 1) + 3 * (sign * dr + 1) + 1
        total = jnp.full((slab, slab), NEG, jnp.float32)
        for dw in (-1, 0, 1):
            value = penalty[slot, first + dw]
            if dt or dr:
                value = jnp.where(inside(dt, dr), value, NEG)
            if minus is not None:
                value = value - minus
            total = jnp.where(step == sign * dw, value, total)
        return total

    def first_pass(slot, blocks, get):
        query, cot, keys, values = own[Q, slot], own[G, slot], get(K), get(V)
        scores = dot_nt(query, keys) * (scale * LOG2E)
        scores = scores + jnp.concatenate([added(slot, dt, dr, 1) for dt, dr in blocks], axis=1)
        highest = jnp.max(scores, axis=1, keepdims=True)
        weights = jnp.exp2(scores - highest)
        total = jnp.sum(weights, axis=1, keepdims=True)
        inverse = 1.0 / total
        out = (dot_nn(weights.astype(jnp.bfloat16), values) * inverse).astype(jnp.bfloat16)
        o_out[slot] = out
        delta = jnp.sum(cot.astype(jnp.float32) * out.astype(jnp.float32), axis=1, keepdims=True)
        slope = (weights * (dot_nt(cot, values) - delta)).astype(jnp.bfloat16)
        dq_out[slot] = (dot_nn(slope, keys) * (inverse * scale)).astype(jnp.bfloat16)
        log_sum = highest + jnp.log2(total)
        held = jnp.where(lane == slot, log_sum, stats_col[...])
        stats_col[...] = jnp.where(lane == slot + 16, delta, held)

    def second_pass(group, slot, blocks, get):
        key, value, queries, cots = own[K, slot], own[V, slot], get(Q), get(G)
        scores = dot_nt(key, queries) * (scale * LOG2E)
        shifts, deltas = [], []
        for dt, dr in blocks:
            source = stats_in.at[dt + 1, dr + 1, group] if dt or dr else stats.at[group]
            shifts.append(added(slot, dt, dr, -1, source[pl.ds(slot, 1), :]))
            deltas.append(source[pl.ds(slot + 16, 1), :])
        probs = jnp.exp2(scores + jnp.concatenate(shifts, axis=1))
        dv_out[slot] = dot_nn(probs.astype(jnp.bfloat16), cots).astype(jnp.bfloat16)
        slope = dot_nt(value, cots) - jnp.concatenate(deltas, axis=1)
        slope = (probs * slope).astype(jnp.bfloat16)
        dk_out[slot] = (dot_nn(slope, queries) * scale).astype(jnp.bfloat16)

    def loop(count, body, pair=1):
        group = count if n == rest else pair if count % 2 == 0 else 1
        if count == group:
            for i in range(count):
                body(i)
        else:
            def several(i, carry):
                for j in range(group):
                    body(group * i + j)
                return carry
            lax.fori_loop(0, count // group, several, 0)

    def slabs(ref, i):
        return lambda array: ref[array, i].reshape(-1, width)

    def first_both():
        loop(n, lambda i: first_pass(i, square, slabs(xb, i)), 2)

    def first_time():
        loop(rest, lambda i: first_pass(n + i, t_line, slabs(xt, i)))

    def first_height():
        loop(rest, lambda i: first_pass(half + i, h_line, slabs(xh, i)))

    def first_alone():
        loop(alone, lambda i: first_pass(half + rest + i, centre, lambda array: own[array, half + rest + i]))

    def second_both():
        loop(n, lambda i: second_pass(0, i, square, slabs(xb, i)), 2)

    def second_time():
        loop(rest, lambda i: second_pass(1, n + i, t_line, slabs(xt, i)))

    def second_height():
        loop(rest, lambda i: second_pass(0, half + i, h_line, slabs(xh, i)))

    def second_alone():
        loop(alone, lambda i: second_pass(0, half + rest + i, centre, lambda array: own[array, half + rest + i]))

    def take_stats(group):
        stats[group] = jnp.transpose(stats_col[...])[: stats.shape[1]]

    if both:
        for array in range(4):
            t_start(array, 0)
            if array < 2:
                h_start(array, 0)
    if lone:
        for array in (K, V):
            t_start(array, 1)
            h_start(array, 1)
    for copy in local:
        copy.wait()
    for ok, copy in fill:
        when(ok, copy.wait)
    first_alone()
    if both:
        relay(K)
        relay(V)
        h_start(Q, 0)
        h_start(G, 0)
        z_relay(K)
        z_relay(V)
    if lone:
        h_wait(K, 1)
        h_wait(V, 1)
        first_height()
    slow = jnp.logical_and(outer, jnp.logical_or(cross[-1], cross[1]))
    if both:
        relay(Q)
        relay(G)
        z_relay(Q)
        z_relay(G)
    if lone:
        for array in (Q, G):
            h_start(array, 1, slow)
    if both:
        for array in (K, V):
            h_wait(array, 0)
            d_wait(array)
        first_both()
    take_stats(0)
    second_alone()
    s_start(0, around)
    if lone:
        for array in (Q, G):
            t_start(array, 1)
            h_start(array, 1, jnp.logical_not(slow))
        t_wait(K, 1)
        t_wait(V, 1)
        first_time()
        take_stats(1)
    s_wait(0, around)
    if lone:
        s_start(1, [(-1, 0), (1, 0)])
    if both:
        for array in (Q, G):
            h_wait(array, 0)
            d_wait(array)
        second_both()
    if lone:
        h_wait(Q, 1)
        h_wait(G, 1)
        second_height()
        t_wait(Q, 1)
        t_wait(G, 1)
        s_wait(1, [(-1, 0), (1, 0)])
        second_time()

    for array in range(4):
        for part in ([0] if both else []) + ([1] if lone else []):
            for d in (-1, 1):
                when(inside(d, 0), lambda array=array, part=part, d=d: t_copy(array, part, d).wait_send())
                when(inside(0, d), lambda array=array, part=part, d=d: h_copy(array, part, d).wait_send())
        if both:
            for e in (-1, 1):
                for d in (-1, 1):
                    ok = jnp.logical_and(inside(e, d), jnp.logical_not(jnp.logical_and(outer, cross[d])))
                    when(ok, lambda array=array, e=e, d=d: d_copy(array, e, d).wait_send())
            for d in (-1, 1):
                for f in (-1, 1):
                    when(jnp.logical_and(inner[f], cross[d]), z_copy(array, f, d).wait_send)
    for dt, dr in around:
        when(inside(dt, dr), lambda dt=dt, dr=dr: s_copy(0, dt, dr).wait_send())
    if lone:
        for d in (-1, 1):
            when(inside(d, 0), lambda d=d: s_copy(1, d, 0).wait_send())


def pack_kernel(
    heads, width, window, mask, k_in, v_in, q_in, g_in, packed, penalty, slots, kind_out
):
    half = heads // 2
    time = [window[0, i] for i in range(heads)]
    height = [window[1, i] for i in range(heads)]
    total = functools.reduce(lambda x, y: x + y, [x * y for x, y in zip(time, height)])
    few, many = total < 2, total > half - 2
    nb = jnp.where(few, 2, jnp.where(many, half, total))
    rest = jnp.where(few, half - 1, jnp.where(many, 1, half - total))
    alone = jnp.where(few, 0, jnp.where(many, half - 2, total))
    lone = half - total
    over = jnp.maximum(lone - rest, 0)
    spare_b = nb - total - 2 * over
    spare_t = jnp.maximum(rest - lone, 0)
    kind_out[0] = jnp.clip(total, 1, half - 1) - 1
    place = lax.broadcasted_iota(jnp.int32, (1, 27), 1)
    moved = (place // 9 != 1, place // 3 % 3 != 1, place % 3 != 1)
    seen = [0, 0, 0, 0]
    for i in range(heads):
        both = time[i] * height[i]
        kinds = [both, time[i] - both, height[i] - both, 1 - time[i] - height[i] + both]
        c = seen
        j = c[3] - alone
        slot = jnp.where(
            both == 1,
            c[0],
            jnp.where(
                time[i] == 1,
                jnp.where(c[1] < rest, nb + c[1], total + c[1] - rest),
                jnp.where(
                    height[i] == 1,
                    jnp.where(c[2] < rest, nb + rest + c[2], total + over + c[2] - rest),
                    jnp.where(
                        j < 0,
                        nb + 2 * rest + c[3],
                        jnp.where(
                            j < spare_b,
                            total + 2 * over + j,
                            jnp.where(j - spare_b < spare_t, nb + lone + j - spare_b, nb + rest + lone + j - spare_b - spare_t),
                        ),
                    ),
                ),
            ),
        )
        seen = [x + k for x, k in zip(c, kinds)]
        slots[i] = slot
        for number, ref in ((K, k_in), (V, v_in), (Q, q_in), (G, g_in)):
            packed[number, slot] = ref[:, i * width : (i + 1) * width]
        row = jnp.where(mask[i : i + 1, :] == 1, 0.0, NEG)
        for axis in range(3):
            row = jnp.where(moved[axis], row + jnp.where(window[axis, i] == 1, 0.0, NEG), row)
        penalty[pl.ds(slot, 1), :] = row


def class_sizes(half):
    return [(2, half - 1, 0)] + [(n, half - n, n) for n in range(2, half - 1)] + [(half, 1, half - 2)]


def spread_kernel(heads, width, slots, o_in, dq_in, dk_in, dv_in, o_out, dq_out, dk_out, dv_out):
    for source, target in ((o_in, o_out), (dq_in, dq_out), (dk_in, dk_out), (dv_in, dv_out)):
        for i in range(heads):
            target[:, i * width : (i + 1) * width] = source[slots[i]]


def on_device(tc, hc, query_vecs, key_vecs, value_vecs, grad_output, tile_window, neighbour_mask):
    slab, features = query_vecs.shape[2:]
    heads = tile_window.shape[0]
    half = heads // 2
    width = features // heads
    vmem = pl.BlockSpec(memory_space=pltpu.VMEM)
    smem = pl.BlockSpec(memory_space=pltpu.SMEM)
    packed = jax.ShapeDtypeStruct((heads, slab, width), jnp.bfloat16)
    dma = pltpu.SemaphoreType.DMA

    def branch(number, sizes):
        n, rest, alone = sizes

        def run(penalty, own):
            return pl.pallas_call(
                functools.partial(fused_kernel, n, rest, alone, tc, hc, slab, width),
                out_shape=(packed,) * 4,
                in_specs=[smem, vmem],
                out_specs=(vmem,) * 4,
                scratch_shapes=[
                    pltpu.VMEM((4, n, 9, slab, width), jnp.bfloat16),
                    pltpu.VMEM((4, rest, 3, slab, width), jnp.bfloat16),
                    pltpu.VMEM((4, rest, 3, slab, width), jnp.bfloat16),
                    pltpu.VMEM((slab, slab), jnp.float32),
                    pltpu.VMEM((2, 32, slab), jnp.float32),
                    pltpu.VMEM((3, 3, 2, 32, slab), jnp.float32),
                    dma((3,)), dma((15,)), dma((4,)),
                    dma((4, 2, 3)), dma((4, 2, 3)),
                    dma((4, 2, 3)), dma((4, 2, 3)),
                    dma((4, 3, 3)), dma((4, 3, 3)),
                    dma((2, 3, 3)), dma((2, 3, 3)),
                ],
                compiler_params=pltpu.CompilerParams(
                    collective_id=number, has_side_effects=True, vmem_limit_bytes=60 * 1024 * 1024
                ),
                name=f"tiles_{n}",
            )(penalty, own)
        return run

    arrays = [x.reshape(slab, features) for x in (key_vecs, value_vecs, query_vecs, grad_output)]
    own, penalty, slots, joint = pl.pallas_call(
        functools.partial(pack_kernel, heads, width),
        out_shape=(
            jax.ShapeDtypeStruct((4, heads, slab, width), jnp.bfloat16),
            jax.ShapeDtypeStruct((heads, 27), jnp.float32),
            jax.ShapeDtypeStruct((heads,), jnp.int32),
            jax.ShapeDtypeStruct((1,), jnp.int32),
        ),
        in_specs=[smem, vmem] + [vmem] * 4,
        out_specs=(vmem, vmem, smem, smem),
        name="pack",
    )(tile_window.T, neighbour_mask, *arrays)
    results = lax.switch(joint[0], [branch(i, x) for i, x in enumerate(class_sizes(half))], penalty, own)
    flat = jax.ShapeDtypeStruct((slab, features), jnp.bfloat16)
    outs = pl.pallas_call(
        functools.partial(spread_kernel, heads, width),
        out_shape=(flat,) * 4,
        in_specs=[smem] + [vmem] * 4,
        out_specs=(vmem,) * 4,
        name="spread",
    )(slots, *results)
    return tuple(x.reshape(1, 1, slab, features) for x in outs)


def solution(mesh):
    split = P("tm", "height", None, None)
    return jax.shard_map(
        functools.partial(on_device, mesh.shape["tm"], mesh.shape["height"]),
        mesh=mesh,
        in_specs=(split,) * 4 + (P(), P()),
        out_specs=(split,) * 4,
        check_vma=False,
    )
```

```python
import functools
import math

import jax
import jax.numpy as jnp
from jax import lax
from jax.experimental import pallas as pl
from jax.experimental.pallas import tpu as pltpu
from jax.sharding import PartitionSpec as P

TILE = 32
NEG = -1e30
K, V, Q, G = 0, 1, 2, 3
MESH = pl.DeviceIdType.MESH
LOG2E = 1.0 / math.log(2.0)


def dot_nt(a, b):
    return lax.dot_general(a, b, (((1,), (1,)), ((), ())), preferred_element_type=jnp.float32)


def dot_nn(a, b):
    return lax.dot_general(a, b, (((1,), (0,)), ((), ())), preferred_element_type=jnp.float32)


def fused_kernel(
    n, rest, tc, hc, slab, width,
    penalty, own, own_h,
    o_out, dq_out, dk_out, dv_out,
    xb, xt, xh, stats_col, stats, stats_in,
    lsend, esend, zsend, tsend, trecv, hsend, hrecv, dsend, drecv, ssend, srecv,
):
    scale = 1.0 / math.sqrt(width)
    half = n + rest
    t = lax.axis_index("tm")
    h = lax.axis_index("height")
    t_near = (jnp.maximum(t - 1, 0), jnp.minimum(t + 1, tc - 1))
    h_near = (jnp.maximum(h - 1, 0), jnp.minimum(h + 1, hc - 1))
    has_t = (t > 0, t < tc - 1)
    has_h = (h > 0, h < hc - 1)
    centre = [(0, 0)]
    h_line = [(0, -1), (0, 1)]
    t_line = [(0, 0), (-1, 0), (1, 0)]
    square = h_line + t_line + [(-1, -1), (-1, 1), (1, -1), (1, 1)]
    at = {x: i for i, x in enumerate(square)}
    around = [x for x in square if x != (0, 0)]

    def inside(dt, dr):
        ok = True
        if dt:
            ok = has_t[(dt + 1) // 2]
        if dr:
            ok = jnp.logical_and(ok, has_h[(dr + 1) // 2])
        return ok

    def when(ok, body):
        if ok is True:
            body()
        else:
            pl.when(ok)(body)

    cross = {-1: h == hc // 2, 1: h == hc // 2 - 1}
    outer = jnp.logical_or(t == 0, t == tc - 1)
    inner = {-1: t == 1, 1: t == tc - 2}
    near_end = jnp.logical_or(inner[-1], inner[1])

    def both_of(a, b):
        return b if a is True else jnp.logical_and(a, b)

    barrier = pltpu.get_barrier_semaphore()
    for dt, dr in around:
        def greet(dt=dt, dr=dr):
            pl.semaphore_signal(barrier, inc=1, device_id=(t + dt, h + dr), device_id_type=MESH)
        when(inside(dt, dr), greet)

    local = []
    if n:
        local.append(pltpu.make_async_copy(own.at[:, pl.ds(0, n)], xb.at[:, :, at[0, 0]], lsend.at[0]))
    if rest:
        local.append(pltpu.make_async_copy(own.at[:, pl.ds(n, rest)], xt.at[:, :, 0], lsend.at[1]))
    for copy in local:
        copy.start()

    fill = []
    for dt, dr in around:
        def add(source, target, number, dt=dt, dr=dr):
            copy = pltpu.make_async_copy(source, target, esend.at[number])
            fill.append((jnp.logical_not(inside(dt, dr)), copy))
        if n:
            add(own.at[:, pl.ds(0, n)], xb.at[:, :, at[dt, dr]], at[dt, dr])
        if rest and dr == 0:
            add(own.at[:, pl.ds(n, rest)], xt.at[:, :, t_line.index((dt, 0))], 10 + dt)
        if rest and dt == 0:
            add(own.at[:, pl.ds(half, rest)], xh.at[:, :, h_line.index((0, dr))], 13 + dr)

        def clear(dt=dt, dr=dr):
            stats_in[dt + 1, dr + 1] = jnp.zeros(stats_in.shape[2:], jnp.float32)
        when(jnp.logical_not(inside(dt, dr)), clear)
    for ok, copy in fill:
        when(ok, copy.start)
    stats_col[...] = jnp.zeros((slab, slab), jnp.float32)

    count_t = has_t[0].astype(jnp.int32) + has_t[1].astype(jnp.int32)
    count_h = has_h[0].astype(jnp.int32) + has_h[1].astype(jnp.int32)
    pl.semaphore_wait(barrier, count_t + count_h + count_t * count_h)

    def t_copy(array, part, d):
        if part == 0:
            source, target = own.at[array, pl.ds(0, n)], xb.at[array, :, at[-d, 0]]
        else:
            source, target = own.at[array, pl.ds(n, rest)], xt.at[array, :, t_line.index((-d, 0))]
        return pltpu.make_async_remote_copy(
            src_ref=source, dst_ref=target,
            send_sem=tsend.at[array, part, d + 1], recv_sem=trecv.at[array, part, 1 - d],
            device_id=(t_near[(d + 1) // 2], h), device_id_type=MESH,
        )

    def h_copy(array, part, d):
        if part == 0:
            source, target = own_h.at[array, pl.ds(0, n)], xb.at[array, :, at[0, -d]]
        else:
            source, target = own_h.at[array, pl.ds(n, rest)], xh.at[array, :, h_line.index((0, -d))]
        return pltpu.make_async_remote_copy(
            src_ref=source, dst_ref=target,
            send_sem=hsend.at[array, part, d + 1], recv_sem=hrecv.at[array, part, 1 - d],
            device_id=(t, h_near[(d + 1) // 2]), device_id_type=MESH,
        )

    def d_copy(array, e, d):
        return pltpu.make_async_remote_copy(
            src_ref=xb.at[array, :, at[e, 0]], dst_ref=xb.at[array, :, at[e, -d]],
            send_sem=dsend.at[array, e + 1, d + 1], recv_sem=drecv.at[array, e + 1, 1 - d],
            device_id=(t, h_near[(d + 1) // 2]), device_id_type=MESH,
        )

    def z_copy(array, f, d):
        return pltpu.make_async_remote_copy(
            src_ref=xb.at[array, :, at[0, d]], dst_ref=xb.at[array, :, at[-f, d]],
            send_sem=zsend.at[array], recv_sem=drecv.at[array, 1 - f, d + 1],
            device_id=(t_near[(f + 1) // 2], h), device_id_type=MESH,
        )

    def s_copy(group, dt, dr):
        return pltpu.make_async_remote_copy(
            src_ref=stats.at[group], dst_ref=stats_in.at[1 - dt, 1 - dr, group],
            send_sem=ssend.at[group, dt + 1, dr + 1], recv_sem=srecv.at[group, 1 - dt, 1 - dr],
            device_id=(t_near[(dt + 1) // 2] if dt else t, h_near[(dr + 1) // 2] if dr else h),
            device_id_type=MESH,
        )

    both, lone = n > 0, rest > 0

    def t_start(array, part):
        for d in (-1, 1):
            when(inside(d, 0), lambda d=d: t_copy(array, part, d).start())

    def h_start(array, part, ok=True):
        for d in (-1, 1):
            when(both_of(ok, inside(0, d)), lambda d=d: h_copy(array, part, d).start())

    def t_wait(array, part):
        for e in (-1, 1):
            when(inside(e, 0), lambda e=e: t_copy(array, part, -e).wait_recv())

    def h_wait(array, part):
        for e in (-1, 1):
            ok = inside(0, e)
            if part == 0:
                ok = both_of(ok, jnp.logical_not(jnp.logical_and(near_end, cross[e])))
            when(ok, lambda e=e: h_copy(array, part, -e).wait_recv())

    def z_relay(array):
        for d in (-1, 1):
            for f in (-1, 1):
                def forward(d=d, f=f):
                    h_copy(array, 0, -d).wait_recv()
                    z_copy(array, f, d).start()
                when(jnp.logical_and(inner[f], cross[d]), forward)

    def relay(array):
        for e in (-1, 1):
            def forward(e=e):
                t_copy(array, 0, -e).wait_recv()
                for d in (-1, 1):
                    ok = jnp.logical_and(inside(0, d), jnp.logical_not(jnp.logical_and(outer, cross[d])))
                    when(ok, lambda d=d: d_copy(array, e, d).start())
            when(inside(e, 0), forward)

    def d_wait(array):
        for e in (-1, 1):
            for d in (-1, 1):
                when(inside(e, d), lambda e=e, d=d: d_copy(array, e, -d).wait_recv())

    def s_start(group, steps):
        for dt, dr in steps:
            when(inside(dt, dr), lambda dt=dt, dr=dr: s_copy(group, dt, dr).start())

    def s_wait(group, steps):
        for dt, dr in steps:
            when(inside(dt, dr), lambda dt=dt, dr=dr: s_copy(group, -dt, -dr).wait_recv())

    row_tile = lax.broadcasted_iota(jnp.int32, (slab, slab), 0) // TILE
    col_tile = lax.broadcasted_iota(jnp.int32, (slab, slab), 1) // TILE
    step = col_tile - row_tile
    lane = lax.broadcasted_iota(jnp.int32, (slab, slab), 1)

    def added(slot, dt, dr, sign, minus=None):
        first = 9 * (sign * dt + 1) + 3 * (sign * dr + 1) + 1
        total = jnp.full((slab, slab), NEG, jnp.float32)
        for dw in (-1, 0, 1):
            value = penalty[slot, first + dw]
            if dt or dr:
                value = jnp.where(inside(dt, dr), value, NEG)
            if minus is not None:
                value = value - minus
            total = jnp.where(step == sign * dw, value, total)
        return total

    def joined(pieces):
        return pieces[0] if len(pieces) == 1 else jnp.concatenate(pieces, axis=1)

    def weighted(rows, segments, array):
        total, start = None, 0
        for blocks, get in segments:
            size = len(blocks) * slab
            part = dot_nn(rows[:, start : start + size], get(array))
            total = part if total is None else total + part
            start += size
        return total

    def first_pass(slot, segments):
        query, cot = own[Q, slot], own[G, slot]
        scores = joined([dot_nt(query, get(K)) for _, get in segments]) * (scale * LOG2E)
        scores = scores + joined([added(slot, dt, dr, 1) for blocks, _ in segments for dt, dr in blocks])
        highest = jnp.max(scores, axis=1, keepdims=True)
        weights = jnp.exp2(scores - highest)
        total = jnp.sum(weights, axis=1, keepdims=True)
        inverse = 1.0 / total
        out = (weighted(weights.astype(jnp.bfloat16), segments, V) * inverse).astype(jnp.bfloat16)
        o_out[slot] = out
        delta = jnp.sum(cot.astype(jnp.float32) * out.astype(jnp.float32), axis=1, keepdims=True)
        slope = joined([dot_nt(cot, get(V)) for _, get in segments])
        slope = (weights * (slope - delta)).astype(jnp.bfloat16)
        dq_out[slot] = (weighted(slope, segments, K) * (inverse * scale)).astype(jnp.bfloat16)
        log_sum = highest + jnp.log2(total)
        held = jnp.where(lane == slot, log_sum, stats_col[...])
        stats_col[...] = jnp.where(lane == slot + 16, delta, held)

    def second_pass(group, slot, segments):
        key, value = own[K, slot], own[V, slot]
        scores = joined([dot_nt(key, get(Q)) for _, get in segments]) * (scale * LOG2E)
        shifts, deltas = [], []
        for blocks, _ in segments:
            for dt, dr in blocks:
                source = stats_in.at[dt + 1, dr + 1, group] if dt or dr else stats.at[group]
                shifts.append(added(slot, dt, dr, -1, source[pl.ds(slot, 1), :]))
                deltas.append(source[pl.ds(slot + 16, 1), :])
        probs = jnp.exp2(scores + joined(shifts))
        dv_out[slot] = weighted(probs.astype(jnp.bfloat16), segments, G).astype(jnp.bfloat16)
        slope = joined([dot_nt(value, get(G)) for _, get in segments]) - joined(deltas)
        slope = (probs * slope).astype(jnp.bfloat16)
        dk_out[slot] = (weighted(slope, segments, Q) * scale).astype(jnp.bfloat16)

    def loop(count, body):
        if n + rest == count or rest:
            for i in range(count):
                body(i)
        elif count:
            lax.fori_loop(0, count, lambda i, c: (body(i), c)[1], 0)

    def slabs(ref, i, size):
        return lambda array: ref[array, i, :size].reshape(size * slab, width)

    def nine(i):
        return [(square, slabs(xb, i, 9))]

    def over_time(i):
        return [(t_line, slabs(xt, i, 3))]

    def over_height(slot, ref, i):
        return [(h_line, slabs(ref, i, 2)), (centre, lambda array: own[array, slot])]

    def take_stats(group):
        stats[group] = jnp.transpose(stats_col[...])[: stats.shape[1]]

    sides = [(-1, 0), (1, 0)]
    for array in range(4):
        t_start(array, 0)
        if array < 2:
            h_start(array, 0)
    if lone:
        for array in (K, V):
            t_start(array, 1)
            h_start(array, 1)
    for copy in local:
        copy.wait()
    for ok, copy in fill:
        when(ok, copy.wait)
    relay(K)
    relay(V)
    h_start(Q, 0)
    h_start(G, 0)
    z_relay(K)
    z_relay(V)
    h_wait(K, 0)
    h_wait(V, 0)
    loop(n, lambda i: first_pass(half + i, over_height(half + i, xb, i)))
    relay(Q)
    z_relay(Q)
    if lone:
        h_wait(K, 1)
        h_wait(V, 1)
        loop(rest, lambda i: first_pass(half + n + i, over_height(half + n + i, xh, i)))
    slow = jnp.logical_and(outer, jnp.logical_or(cross[-1], cross[1]))
    if lone:
        for array in (Q, G):
            h_start(array, 1, slow)
    d_wait(K)
    d_wait(V)
    loop(n, lambda i: first_pass(i, nine(i)))
    take_stats(0)
    s_start(0, around)
    relay(G)
    z_relay(G)
    if lone:
        for array in (Q, G):
            t_start(array, 1)
            h_start(array, 1, jnp.logical_not(slow))
        t_wait(K, 1)
        t_wait(V, 1)
        loop(rest, lambda i: first_pass(n + i, over_time(i)))
        take_stats(1)
    s_wait(0, around)
    if lone:
        s_start(1, sides)
    h_wait(Q, 0)
    h_wait(G, 0)
    loop(n, lambda i: second_pass(0, half + i, over_height(half + i, xb, i)))
    d_wait(Q)
    d_wait(G)
    loop(n, lambda i: second_pass(0, i, nine(i)))
    if lone:
        h_wait(Q, 1)
        h_wait(G, 1)
        loop(rest, lambda i: second_pass(0, half + n + i, over_height(half + n + i, xh, i)))
        t_wait(Q, 1)
        t_wait(G, 1)
        s_wait(1, sides)
        loop(rest, lambda i: second_pass(1, n + i, over_time(i)))

    for array in range(4):
        for part in ([0] if both else []) + ([1] if lone else []):
            for d in (-1, 1):
                when(inside(d, 0), lambda array=array, part=part, d=d: t_copy(array, part, d).wait_send())
                when(inside(0, d), lambda array=array, part=part, d=d: h_copy(array, part, d).wait_send())
        if both:
            for e in (-1, 1):
                for d in (-1, 1):
                    ok = jnp.logical_and(inside(e, d), jnp.logical_not(jnp.logical_and(outer, cross[d])))
                    when(ok, lambda array=array, e=e, d=d: d_copy(array, e, d).wait_send())
            for d in (-1, 1):
                for f in (-1, 1):
                    when(jnp.logical_and(inner[f], cross[d]), z_copy(array, f, d).wait_send)
    for dt, dr in around:
        when(inside(dt, dr), lambda dt=dt, dr=dr: s_copy(0, dt, dr).wait_send())
    if lone:
        for d in (-1, 1):
            when(inside(d, 0), lambda d=d: s_copy(1, d, 0).wait_send())


def pack_kernel(
    heads, width, most, window, mask, k_in, v_in, q_in, g_in, packed, packed_h, penalty, slots, kind_out
):
    half = heads // 2
    time = [window[0, i] for i in range(heads)]
    height = [window[1, i] for i in range(heads)]
    total = functools.reduce(lambda x, y: x + y, [x * y for x, y in zip(time, height)])
    kind_out[0] = jnp.where(total > most, 1, 0)
    place = lax.broadcasted_iota(jnp.int32, (1, 27), 1)
    moved = (place // 9 != 1, place // 3 % 3 != 1, place % 3 != 1)
    seen = [0, total, half + total, half]
    for i in range(heads):
        both = time[i] * height[i]
        kinds = [both, time[i] - both, height[i] - both, 1 - time[i] - height[i] + both]
        slot = sum(k * c for k, c in zip(kinds, seen))
        slot_h = jnp.where(height[i] == 1, jnp.where(time[i] == 1, seen[0], seen[2] - half), half)
        seen = [c + k for k, c in zip(kinds, seen)]
        slots[i] = slot
        for number, ref in ((K, k_in), (V, v_in), (Q, q_in), (G, g_in)):
            value = ref[:, i * width : (i + 1) * width]
            packed[number, slot] = value
            packed_h[number, slot_h] = value
        row = jnp.where(mask[i : i + 1, :] == 1, 0.0, NEG)
        for axis in range(3):
            row = jnp.where(moved[axis], row + jnp.where(window[axis, i] == 1, 0.0, NEG), row)
        penalty[pl.ds(slot, 1), :] = row


def spread_kernel(heads, width, slots, o_in, dq_in, dk_in, dv_in, o_out, dq_out, dk_out, dv_out):
    for source, target in ((o_in, o_out), (dq_in, dq_out), (dk_in, dk_out), (dv_in, dv_out)):
        for i in range(heads):
            target[:, i * width : (i + 1) * width] = source[slots[i]]


def on_device(tc, hc, query_vecs, key_vecs, value_vecs, grad_output, tile_window, neighbour_mask):
    slab, features = query_vecs.shape[2:]
    heads = tile_window.shape[0]
    half = heads // 2
    width = features // heads
    vmem = pl.BlockSpec(memory_space=pltpu.VMEM)
    smem = pl.BlockSpec(memory_space=pltpu.SMEM)
    packed = jax.ShapeDtypeStruct((heads, slab, width), jnp.bfloat16)
    dma = pltpu.SemaphoreType.DMA

    def branch(number, n):
        rest = half - n

        def run(penalty, own, own_h):
            return pl.pallas_call(
                functools.partial(fused_kernel, n, rest, tc, hc, slab, width),
                out_shape=(packed,) * 4,
                in_specs=[smem, vmem, vmem],
                out_specs=(vmem,) * 4,
                scratch_shapes=[
                    pltpu.VMEM((4, n, 9, slab, width), jnp.bfloat16),
                    pltpu.VMEM((4, max(rest, 1), 3, slab, width), jnp.bfloat16),
                    pltpu.VMEM((4, max(rest, 1), 2, slab, width), jnp.bfloat16),
                    pltpu.VMEM((slab, slab), jnp.float32),
                    pltpu.VMEM((2, 32, slab), jnp.float32),
                    pltpu.VMEM((3, 3, 2, 32, slab), jnp.float32),
                    dma((3,)), dma((15,)), dma((4,)),
                    dma((4, 2, 3)), dma((4, 2, 3)),
                    dma((4, 2, 3)), dma((4, 2, 3)),
                    dma((4, 3, 3)), dma((4, 3, 3)),
                    dma((2, 3, 3)), dma((2, 3, 3)),
                ],
                compiler_params=pltpu.CompilerParams(
                    collective_id=number, has_side_effects=True, vmem_limit_bytes=40 * 1024 * 1024
                ),
                name=f"tiles_{n}",
            )(penalty, own, own_h)
        return run

    arrays = [x.reshape(slab, features) for x in (key_vecs, value_vecs, query_vecs, grad_output)]
    most = 2 * half // 3
    own, own_h, penalty, slots, joint = pl.pallas_call(
        functools.partial(pack_kernel, heads, width, most),
        out_shape=(
            jax.ShapeDtypeStruct((4, heads, slab, width), jnp.bfloat16),
            jax.ShapeDtypeStruct((4, half + 1, slab, width), jnp.bfloat16),
            jax.ShapeDtypeStruct((heads, 27), jnp.float32),
            jax.ShapeDtypeStruct((heads,), jnp.int32),
            jax.ShapeDtypeStruct((1,), jnp.int32),
        ),
        in_specs=[smem, vmem] + [vmem] * 4,
        out_specs=(vmem, vmem, vmem, smem, smem),
        name="pack",
    )(tile_window.T, neighbour_mask, *arrays)
    results = lax.switch(joint[0], [branch(0, most), branch(1, half)], penalty, own, own_h)
    flat = jax.ShapeDtypeStruct((slab, features), jnp.bfloat16)
    outs = pl.pallas_call(
        functools.partial(spread_kernel, heads, width),
        out_shape=(flat,) * 4,
        in_specs=[smem] + [vmem] * 4,
        out_specs=(vmem,) * 4,
        name="spread",
    )(slots, *results)
    return tuple(x.reshape(1, 1, slab, features) for x in outs)


def solution(mesh):
    split = P("tm", "height", None, None)
    return jax.shard_map(
        functools.partial(on_device, mesh.shape["tm"], mesh.shape["height"]),
        mesh=mesh,
        in_specs=(split,) * 4 + (P(), P()),
        out_specs=(split,) * 4,
        check_vma=False,
    )
```

```python
import functools
import math

import jax
import jax.numpy as jnp
from jax import lax
from jax.experimental import pallas as pl
from jax.experimental.pallas import tpu as pltpu
from jax.sharding import PartitionSpec as P

TILE = 32
NEG = -1e30
K, V, Q, G = 0, 1, 2, 3
MESH = pl.DeviceIdType.MESH
LOG2E = 1.0 / math.log(2.0)


def dot_nt(a, b):
    return lax.dot_general(a, b, (((1,), (1,)), ((), ())), preferred_element_type=jnp.float32)


def dot_nn(a, b):
    return lax.dot_general(a, b, (((1,), (0,)), ((), ())), preferred_element_type=jnp.float32)


def fused_kernel(
    n, rest, tc, hc, slab, width,
    penalty, own, own_h,
    o_out, dq_out, dk_out, dv_out,
    xb, xt, xh, stats_col, stats, stats_in,
    lsend, esend, zsend, tsend, trecv, hsend, hrecv, dsend, drecv, ssend, srecv,
):
    scale = 1.0 / math.sqrt(width)
    half = n + rest
    t = lax.axis_index("tm")
    h = lax.axis_index("height")
    t_near = (jnp.maximum(t - 1, 0), jnp.minimum(t + 1, tc - 1))
    h_near = (jnp.maximum(h - 1, 0), jnp.minimum(h + 1, hc - 1))
    has_t = (t > 0, t < tc - 1)
    has_h = (h > 0, h < hc - 1)
    centre = [(0, 0)]
    h_line = [(0, -1), (0, 1)]
    t_line = [(0, 0), (-1, 0), (1, 0)]
    square = h_line + t_line + [(-1, -1), (-1, 1), (1, -1), (1, 1)]
    at = {x: i for i, x in enumerate(square)}
    around = [x for x in square if x != (0, 0)]

    def inside(dt, dr):
        ok = True
        if dt:
            ok = has_t[(dt + 1) // 2]
        if dr:
            ok = jnp.logical_and(ok, has_h[(dr + 1) // 2])
        return ok

    def when(ok, body):
        if ok is True:
            body()
        else:
            pl.when(ok)(body)

    cross = {-1: h == hc // 2, 1: h == hc // 2 - 1}
    outer = jnp.logical_or(t == 0, t == tc - 1)
    inner = {-1: t == 1, 1: t == tc - 2}
    near_end = jnp.logical_or(inner[-1], inner[1])

    held = jnp.logical_and(t == tc // 2, jnp.logical_and(h >= hc // 2 - 2, h < hc // 2 + 2))

    def both_of(a, b):
        return b if a is True else jnp.logical_and(a, b)

    barrier = pltpu.get_barrier_semaphore()
    for dt, dr in around:
        def greet(dt=dt, dr=dr):
            pl.semaphore_signal(barrier, inc=1, device_id=(t + dt, h + dr), device_id_type=MESH)
        when(inside(dt, dr), greet)

    local = []
    if n:
        local.append(pltpu.make_async_copy(own.at[:, pl.ds(0, n)], xb.at[:, :, at[0, 0]], lsend.at[0]))
    if rest:
        local.append(pltpu.make_async_copy(own.at[:, pl.ds(n, rest)], xt.at[:, :, 0], lsend.at[1]))
    for copy in local:
        copy.start()

    fill = []
    for dt, dr in around:
        def add(source, target, number, dt=dt, dr=dr):
            copy = pltpu.make_async_copy(source, target, esend.at[number])
            fill.append((jnp.logical_not(inside(dt, dr)), copy))
        if n:
            add(own.at[:, pl.ds(0, n)], xb.at[:, :, at[dt, dr]], at[dt, dr])
        if rest and dr == 0:
            add(own.at[:, pl.ds(n, rest)], xt.at[:, :, t_line.index((dt, 0))], 10 + dt)
        if rest and dt == 0:
            add(own.at[:, pl.ds(half, rest)], xh.at[:, :, h_line.index((0, dr))], 13 + dr)

        def clear(dt=dt, dr=dr):
            stats_in[dt + 1, dr + 1] = jnp.zeros(stats_in.shape[2:], jnp.float32)
        when(jnp.logical_not(inside(dt, dr)), clear)
    for ok, copy in fill:
        when(ok, copy.start)
    stats_col[...] = jnp.zeros((slab, slab), jnp.float32)

    count_t = has_t[0].astype(jnp.int32) + has_t[1].astype(jnp.int32)
    count_h = has_h[0].astype(jnp.int32) + has_h[1].astype(jnp.int32)
    pl.semaphore_wait(barrier, count_t + count_h + count_t * count_h)

    def t_copy(array, part, d):
        if part == 0:
            source, target = own.at[array, pl.ds(0, n)], xb.at[array, :, at[-d, 0]]
        else:
            source, target = own.at[array, pl.ds(n, rest)], xt.at[array, :, t_line.index((-d, 0))]
        return pltpu.make_async_remote_copy(
            src_ref=source, dst_ref=target,
            send_sem=tsend.at[array, part, d + 1], recv_sem=trecv.at[array, part, 1 - d],
            device_id=(t_near[(d + 1) // 2], h), device_id_type=MESH,
        )

    def h_copy(array, part, d):
        if part == 0:
            source, target = own_h.at[array, pl.ds(0, n)], xb.at[array, :, at[0, -d]]
        else:
            source, target = own_h.at[array, pl.ds(n, rest)], xh.at[array, :, h_line.index((0, -d))]
        return pltpu.make_async_remote_copy(
            src_ref=source, dst_ref=target,
            send_sem=hsend.at[array, part, d + 1], recv_sem=hrecv.at[array, part, 1 - d],
            device_id=(t, h_near[(d + 1) // 2]), device_id_type=MESH,
        )

    def d_copy(array, e, d):
        return pltpu.make_async_remote_copy(
            src_ref=xb.at[array, :, at[e, 0]], dst_ref=xb.at[array, :, at[e, -d]],
            send_sem=dsend.at[array, e + 1, d + 1], recv_sem=drecv.at[array, e + 1, 1 - d],
            device_id=(t, h_near[(d + 1) // 2]), device_id_type=MESH,
        )

    def z_copy(array, f, d):
        return pltpu.make_async_remote_copy(
            src_ref=xb.at[array, :, at[0, d]], dst_ref=xb.at[array, :, at[-f, d]],
            send_sem=zsend.at[array], recv_sem=drecv.at[array, 1 - f, d + 1],
            device_id=(t_near[(f + 1) // 2], h), device_id_type=MESH,
        )

    def s_copy(group, dt, dr):
        return pltpu.make_async_remote_copy(
            src_ref=stats.at[group], dst_ref=stats_in.at[1 - dt, 1 - dr, group],
            send_sem=ssend.at[group, dt + 1, dr + 1], recv_sem=srecv.at[group, 1 - dt, 1 - dr],
            device_id=(t_near[(dt + 1) // 2] if dt else t, h_near[(dr + 1) // 2] if dr else h),
            device_id_type=MESH,
        )

    both, lone = n > 0, rest > 0

    def t_start(array, part, ok=True, late=None):
        for d in (-1, 1):
            go = both_of(ok, inside(d, 0))
            if late is not None and d == -1:
                go = jnp.logical_and(go, held if late else jnp.logical_not(held))
            if not late or d == -1:
                when(go, lambda d=d: t_copy(array, part, d).start())

    def h_start(array, part, early=False):
        for d in (-1, 1):
            shared = jnp.logical_and(outer, cross[d])
            ok = shared if early else jnp.logical_and(inside(0, d), jnp.logical_not(shared))
            when(ok, lambda d=d: h_copy(array, part, d).start())

    def t_wait(array, part):
        for e in (-1, 1):
            when(inside(e, 0), lambda e=e: t_copy(array, part, -e).wait_recv())

    def h_wait(array, part):
        for e in (-1, 1):
            ok = inside(0, e)
            if part == 0:
                ok = both_of(ok, jnp.logical_not(jnp.logical_and(near_end, cross[e])))
            when(ok, lambda e=e: h_copy(array, part, -e).wait_recv())

    def z_relay(array):
        for d in (-1, 1):
            for f in (-1, 1):
                def forward(d=d, f=f):
                    h_copy(array, 0, -d).wait_recv()
                    z_copy(array, f, d).start()
                when(jnp.logical_and(inner[f], cross[d]), forward)

    def relay(array, here=True):
        for e in (-1, 1):
            def forward(e=e):
                t_copy(array, 0, -e).wait_recv()
                for d in (-1, 1):
                    ok = jnp.logical_and(inside(0, d), jnp.logical_not(jnp.logical_and(outer, cross[d])))
                    when(ok, lambda d=d: d_copy(array, e, d).start())
            when(both_of(here, inside(e, 0)), forward)

    def d_wait(array):
        for e in (-1, 1):
            for d in (-1, 1):
                when(inside(e, d), lambda e=e, d=d: d_copy(array, e, -d).wait_recv())

    def s_start(group, steps):
        for dt, dr in steps:
            when(inside(dt, dr), lambda dt=dt, dr=dr: s_copy(group, dt, dr).start())

    def s_wait(group, steps):
        for dt, dr in steps:
            when(inside(dt, dr), lambda dt=dt, dr=dr: s_copy(group, -dt, -dr).wait_recv())

    row_tile = lax.broadcasted_iota(jnp.int32, (slab, slab), 0) // TILE
    col_tile = lax.broadcasted_iota(jnp.int32, (slab, slab), 1) // TILE
    step = col_tile - row_tile
    lane = lax.broadcasted_iota(jnp.int32, (slab, slab), 1)

    def added(slot, dt, dr, sign, minus=None):
        first = 9 * (sign * dt + 1) + 3 * (sign * dr + 1) + 1
        total = jnp.full((slab, slab), NEG, jnp.float32)
        for dw in (-1, 0, 1):
            value = penalty[slot, first + dw]
            if dt or dr:
                value = jnp.where(inside(dt, dr), value, NEG)
            if minus is not None:
                value = value - minus
            total = jnp.where(step == sign * dw, value, total)
        return total

    def joined(pieces):
        return pieces[0] if len(pieces) == 1 else jnp.concatenate(pieces, axis=1)

    def weighted(rows, segments, array):
        total, start = None, 0
        for blocks, get in segments:
            size = len(blocks) * slab
            part = dot_nn(rows[:, start : start + size], get(array))
            total = part if total is None else total + part
            start += size
        return total

    def first_pass(slot, segments):
        query, cot = own[Q, slot], own[G, slot]
        scores = joined([dot_nt(query, get(K)) for _, get in segments]) * (scale * LOG2E)
        scores = scores + joined([added(slot, dt, dr, 1) for blocks, _ in segments for dt, dr in blocks])
        highest = jnp.max(scores, axis=1, keepdims=True)
        weights = jnp.exp2(scores - highest)
        total = jnp.sum(weights, axis=1, keepdims=True)
        inverse = 1.0 / total
        out = (weighted(weights.astype(jnp.bfloat16), segments, V) * inverse).astype(jnp.bfloat16)
        o_out[slot] = out
        delta = jnp.sum(cot.astype(jnp.float32) * out.astype(jnp.float32), axis=1, keepdims=True)
        slope = joined([dot_nt(cot, get(V)) for _, get in segments])
        slope = (weights * (slope - delta)).astype(jnp.bfloat16)
        dq_out[slot] = (weighted(slope, segments, K) * (inverse * scale)).astype(jnp.bfloat16)
        log_sum = highest + jnp.log2(total)
        held = jnp.where(lane == slot, log_sum, stats_col[...])
        stats_col[...] = jnp.where(lane == slot + 16, delta, held)

    def second_pass(group, slot, segments):
        key, value = own[K, slot], own[V, slot]
        scores = joined([dot_nt(key, get(Q)) for _, get in segments]) * (scale * LOG2E)
        shifts, deltas = [], []
        for blocks, _ in segments:
            for dt, dr in blocks:
                source = stats_in.at[dt + 1, dr + 1, group] if dt or dr else stats.at[group]
                shifts.append(added(slot, dt, dr, -1, source[pl.ds(slot, 1), :]))
                deltas.append(source[pl.ds(slot + 16, 1), :])
        probs = jnp.exp2(scores + joined(shifts))
        dv_out[slot] = weighted(probs.astype(jnp.bfloat16), segments, G).astype(jnp.bfloat16)
        slope = joined([dot_nt(value, get(G)) for _, get in segments]) - joined(deltas)
        slope = (probs * slope).astype(jnp.bfloat16)
        dk_out[slot] = (weighted(slope, segments, Q) * scale).astype(jnp.bfloat16)

    def loop(count, body):
        if n + rest == count or rest:
            for i in range(count):
                body(i)
        elif count:
            lax.fori_loop(0, count, lambda i, c: (body(i), c)[1], 0)

    def slabs(ref, i, size):
        return lambda array: ref[array, i, :size].reshape(size * slab, width)

    def nine(i):
        return [(square, slabs(xb, i, 9))]

    def over_time(i):
        return [(t_line, slabs(xt, i, 3))]

    def over_height(slot, ref, i):
        return [(h_line, slabs(ref, i, 2)), (centre, lambda array: own[array, slot])]

    def take_stats(group):
        stats[group] = jnp.transpose(stats_col[...])[: stats.shape[1]]

    sides = [(-1, 0), (1, 0)]
    slow = jnp.logical_and(outer, jnp.logical_or(cross[-1], cross[1]))
    prompt = jnp.logical_not(slow)
    for arrays in ((K, V), (Q, G)):
        for part in (0, 1) if lone else (0,):
            for array in arrays:
                h_start(array, part, True)
    for array in range(4):
        t_start(array, 0, late=None if array < 2 else False)
        if array < 2:
            h_start(array, 0)
    if lone:
        for array in (K, V):
            t_start(array, 1, late=False)
            h_start(array, 1)
    for copy in local:
        copy.wait()
    for ok, copy in fill:
        when(ok, copy.wait)
    relay(K)
    relay(V)
    h_start(Q, 0)
    h_start(G, 0)
    if lone:
        for array in (Q, G):
            t_start(array, 1, slow)
    relay(Q, slow)
    relay(G, slow)
    z_relay(K)
    z_relay(V)
    h_wait(K, 0)
    h_wait(V, 0)
    loop(n, lambda i: first_pass(half + i, over_height(half + i, xb, i)))
    t_start(Q, 0, late=True)
    t_start(G, 0, late=True)
    if lone:
        t_start(K, 1, late=True)
        t_start(V, 1, late=True)
    relay(Q, prompt)
    z_relay(Q)
    if lone:
        h_wait(K, 1)
        h_wait(V, 1)
        loop(rest, lambda i: first_pass(half + n + i, over_height(half + n + i, xh, i)))
    d_wait(K)
    d_wait(V)
    loop(n, lambda i: first_pass(i, nine(i)))
    take_stats(0)
    s_start(0, around)
    relay(G, prompt)
    z_relay(G)
    if lone:
        for array in (Q, G):
            t_start(array, 1, prompt)
            h_start(array, 1)
        t_wait(K, 1)
        t_wait(V, 1)
        loop(rest, lambda i: first_pass(n + i, over_time(i)))
        take_stats(1)
    s_wait(0, around)
    if lone:
        s_start(1, sides)
    h_wait(Q, 0)
    h_wait(G, 0)
    loop(n, lambda i: second_pass(0, half + i, over_height(half + i, xb, i)))
    d_wait(Q)
    d_wait(G)
    loop(n, lambda i: second_pass(0, i, nine(i)))
    if lone:
        h_wait(Q, 1)
        h_wait(G, 1)
        loop(rest, lambda i: second_pass(0, half + n + i, over_height(half + n + i, xh, i)))
        t_wait(Q, 1)
        t_wait(G, 1)
        s_wait(1, sides)
        loop(rest, lambda i: second_pass(1, n + i, over_time(i)))

    for array in range(4):
        for part in ([0] if both else []) + ([1] if lone else []):
            for d in (-1, 1):
                when(inside(d, 0), lambda array=array, part=part, d=d: t_copy(array, part, d).wait_send())
                when(inside(0, d), lambda array=array, part=part, d=d: h_copy(array, part, d).wait_send())
        if both:
            for e in (-1, 1):
                for d in (-1, 1):
                    ok = jnp.logical_and(inside(e, d), jnp.logical_not(jnp.logical_and(outer, cross[d])))
                    when(ok, lambda array=array, e=e, d=d: d_copy(array, e, d).wait_send())
            for d in (-1, 1):
                for f in (-1, 1):
                    when(jnp.logical_and(inner[f], cross[d]), z_copy(array, f, d).wait_send)
    for dt, dr in around:
        when(inside(dt, dr), lambda dt=dt, dr=dr: s_copy(0, dt, dr).wait_send())
    if lone:
        for d in (-1, 1):
            when(inside(d, 0), lambda d=d: s_copy(1, d, 0).wait_send())


def pack_kernel(
    heads, width, most, window, mask, k_in, v_in, q_in, g_in, packed, packed_h, penalty, slots, kind_out
):
    half = heads // 2
    time = [window[0, i] for i in range(heads)]
    height = [window[1, i] for i in range(heads)]
    total = functools.reduce(lambda x, y: x + y, [x * y for x, y in zip(time, height)])
    kind_out[0] = jnp.where(total > most, 1, 0)
    place = lax.broadcasted_iota(jnp.int32, (1, 27), 1)
    moved = (place // 9 != 1, place // 3 % 3 != 1, place % 3 != 1)
    seen = [0, total, half + total, half]
    for i in range(heads):
        both = time[i] * height[i]
        kinds = [both, time[i] - both, height[i] - both, 1 - time[i] - height[i] + both]
        slot = sum(k * c for k, c in zip(kinds, seen))
        slot_h = jnp.where(height[i] == 1, jnp.where(time[i] == 1, seen[0], seen[2] - half), half)
        seen = [c + k for k, c in zip(kinds, seen)]
        slots[i] = slot
        for number, ref in ((K, k_in), (V, v_in), (Q, q_in), (G, g_in)):
            value = ref[:, i * width : (i + 1) * width]
            packed[number, slot] = value
            packed_h[number, slot_h] = value
        row = jnp.where(mask[i : i + 1, :] == 1, 0.0, NEG)
        for axis in range(3):
            row = jnp.where(moved[axis], row + jnp.where(window[axis, i] == 1, 0.0, NEG), row)
        penalty[pl.ds(slot, 1), :] = row


def spread_kernel(heads, width, slots, o_in, dq_in, dk_in, dv_in, o_out, dq_out, dk_out, dv_out):
    for source, target in ((o_in, o_out), (dq_in, dq_out), (dk_in, dk_out), (dv_in, dv_out)):
        for i in range(heads):
            target[:, i * width : (i + 1) * width] = source[slots[i]]


def on_device(tc, hc, query_vecs, key_vecs, value_vecs, grad_output, tile_window, neighbour_mask):
    slab, features = query_vecs.shape[2:]
    heads = tile_window.shape[0]
    half = heads // 2
    width = features // heads
    vmem = pl.BlockSpec(memory_space=pltpu.VMEM)
    smem = pl.BlockSpec(memory_space=pltpu.SMEM)
    packed = jax.ShapeDtypeStruct((heads, slab, width), jnp.bfloat16)
    dma = pltpu.SemaphoreType.DMA

    def branch(number, n):
        rest = half - n

        def run(penalty, own, own_h):
            return pl.pallas_call(
                functools.partial(fused_kernel, n, rest, tc, hc, slab, width),
                out_shape=(packed,) * 4,
                in_specs=[smem, vmem, vmem],
                out_specs=(vmem,) * 4,
                scratch_shapes=[
                    pltpu.VMEM((4, n, 9, slab, width), jnp.bfloat16),
                    pltpu.VMEM((4, max(rest, 1), 3, slab, width), jnp.bfloat16),
                    pltpu.VMEM((4, max(rest, 1), 2, slab, width), jnp.bfloat16),
                    pltpu.VMEM((slab, slab), jnp.float32),
                    pltpu.VMEM((2, 32, slab), jnp.float32),
                    pltpu.VMEM((3, 3, 2, 32, slab), jnp.float32),
                    dma((3,)), dma((15,)), dma((4,)),
                    dma((4, 2, 3)), dma((4, 2, 3)),
                    dma((4, 2, 3)), dma((4, 2, 3)),
                    dma((4, 3, 3)), dma((4, 3, 3)),
                    dma((2, 3, 3)), dma((2, 3, 3)),
                ],
                compiler_params=pltpu.CompilerParams(
                    collective_id=number, has_side_effects=True, vmem_limit_bytes=40 * 1024 * 1024
                ),
                name=f"tiles_{n}",
            )(penalty, own, own_h)
        return run

    arrays = [x.reshape(slab, features) for x in (key_vecs, value_vecs, query_vecs, grad_output)]
    most = 2 * half // 3
    own, own_h, penalty, slots, joint = pl.pallas_call(
        functools.partial(pack_kernel, heads, width, most),
        out_shape=(
            jax.ShapeDtypeStruct((4, heads, slab, width), jnp.bfloat16),
            jax.ShapeDtypeStruct((4, half + 1, slab, width), jnp.bfloat16),
            jax.ShapeDtypeStruct((heads, 27), jnp.float32),
            jax.ShapeDtypeStruct((heads,), jnp.int32),
            jax.ShapeDtypeStruct((1,), jnp.int32),
        ),
        in_specs=[smem, vmem] + [vmem] * 4,
        out_specs=(vmem, vmem, vmem, smem, smem),
        name="pack",
    )(tile_window.T, neighbour_mask, *arrays)
    results = lax.switch(joint[0], [branch(0, most), branch(1, half)], penalty, own, own_h)
    flat = jax.ShapeDtypeStruct((slab, features), jnp.bfloat16)
    outs = pl.pallas_call(
        functools.partial(spread_kernel, heads, width),
        out_shape=(flat,) * 4,
        in_specs=[smem] + [vmem] * 4,
        out_specs=(vmem,) * 4,
        name="spread",
    )(slots, *results)
    return tuple(x.reshape(1, 1, slab, features) for x in outs)


def solution(mesh):
    split = P("tm", "height", None, None)
    return jax.shard_map(
        functools.partial(on_device, mesh.shape["tm"], mesh.shape["height"]),
        mesh=mesh,
        in_specs=(split,) * 4 + (P(), P()),
        out_specs=(split,) * 4,
        check_vma=False,
    )
```
